256 devices in a mesh: expert: 64 (over z, x, core), dp: 4 (over y).
Axes of the slice: x: 4, y: 4, z: 8, core: 2. Of those that a mesh axis runs over, the one named last changes fastest.
Arguments:
- tokens: bfloat16 [14336, 2048], P(('expert', 'dp')), may hold values from -6 to 6
- cotangent: bfloat16 [14336, 2048], P(('expert', 'dp')), may hold values from -6 to 6
- expert_ids: int32 [14336, 8], P(('expert', 'dp')), may hold values from 0 to 63, all different within a row; in each aligned block of 56 rows (0 to 55, 56 to 111, ...) at most 8 rows name the same one
- combine: bfloat16 [14336, 8], P(('expert', 'dp')), may hold values from 0.019897461 to 0.5
- gate_up: bfloat16 [64, 2048, 1536], P('expert'), may hold values from -0.125 to 0.125
- down_proj: bfloat16 [64, 2048, 768], P('expert'), may hold values from -0.21875 to 0.21875
Outputs:
- grad_tokens: bfloat16 [14336, 2048], P(('expert', 'dp'))
- grad_combine: bfloat16 [14336, 8], P(('expert', 'dp'))
- grad_gate_up: bfloat16 [64, 2048, 1536], P('expert', 'dp')
- grad_down: bfloat16 [64, 2048, 768], P('expert', 'dp')
The draws below stay inside these ranges and needn't reach their ends.
Inputs may be any that keep to these rules, and one draw needn't show every extreme that they name: `expert_ids`: each token names 8 different experts. Among the 56 tokens of one device (aligned blocks of rows) no expert is named more than 8 times, and in every draw some device names some expert exactly 8 times.
All inputs are finite; a program needn't handle non-finite values.
Results may differ from the reference program's by a relative error of at most 0.015.
Values may be sent and summed in bfloat16 or wider, within the bound.
A program may use at most 128 MiB of HBM per device.

```python
import math
import jax
import jax.numpy as jnp
import numpy as np
from jax import lax

D = 2048
H = 768
TOP = 8
TOK_DEV = 56
EXPERTS = 64
CAP = 8
TOKENS = 14336
N_EXPERT = 64
N_DP = 4


def levels(stream_key, dims, cuts, low, high):
    gain = 1.0
    for position, blocks in cuts:
        steps = jax.random.uniform(jax.random.fold_in(jax.random.fold_in(stream_key, 6), position), (blocks,), jnp.float32, low / len(cuts), high / len(cuts))
        gain = gain * jnp.repeat(jnp.exp(steps), dims[position] // blocks).reshape((-1,) + (1,) * (len(dims) - 1 - position))
    return gain


def shared_out(stream_key, own, number, rows, amount, top, bound, skew):
    ranking = jax.random.permutation(stream_key, amount)
    crowded, usual = load_shares(amount, rows * top, bound, skew, True), load_shares(amount, rows * top, bound, skew, False)
    places = jnp.arange(amount)

    def named(lengths, offset_by):
        used = int((lengths > 0).sum())
        fixed = max(1, used // 4)
        passed = fixed + (places - fixed + offset_by * (used - fixed)) % max(1, amount - fixed)
        return jnp.zeros((amount,), jnp.int32).at[ranking[jnp.where(places < fixed, places, passed)]].set(jnp.asarray(lengths, jnp.int32))

    lengths = jnp.where(number % 4 == 0, named(crowded, number // 4), named(usual, number - number // 4 - 1))
    mixed = jax.random.permutation(jax.random.fold_in(own, 3), amount)
    donor, taker = mixed[0:amount // 2 * 2:2], mixed[1:amount // 2 * 2:2]
    slack = jnp.minimum(lengths[donor] - 1, bound - lengths[taker]) // 2
    slack = jnp.where((donor == ranking[0]) | (taker == ranking[0]) | (lengths[taker] == 0), 0, jnp.maximum(slack, 0))
    passed = jax.random.randint(jax.random.fold_in(own, 4), (amount // 2,), 0, 1 << 20) % (slack + 1)
    lengths = lengths.at[donor].add(-passed).at[taker].add(passed)
    labels = jnp.searchsorted(jnp.cumsum(lengths), jnp.arange(rows * top), side="right").astype(jnp.int32)
    listing = labels.reshape(top, rows).T
    listing = listing[jax.random.permutation(jax.random.fold_in(own, 1), rows)]
    offset_by = jax.random.randint(jax.random.fold_in(own, 2), (rows, 1), 0, top)
    return jnp.take_along_axis(listing, (jnp.arange(top)[None, :] + offset_by) % top, axis=1)


def load_shares(number_of, total, most, skew, full):
    weights = [(1 << 20) // math.isqrt(rank ** skew) + 1 for rank in range(1, number_of + 1)]
    largest = most if full else min(most, max(-(-total // number_of), total * weights[0] // sum(weights)))
    least = 1 if total - largest >= number_of - 1 else 0
    given, surplus = [largest] + [least] * (number_of - 1), total - largest - least * (number_of - 1)
    while surplus > 0:
        free = [i for i in range(1, number_of) if given[i] < largest] or [i for i in range(1, number_of) if given[i] < most]
        mass, budget = sum([weights[i] for i in free]), surplus
        for i in free:
            more = min(most - given[i], max(1, budget * weights[i] // mass), surplus)
            given[i] = given[i] + more
            surplus = surplus - more
    return np.array(given)


def noise(own_key, extent, width, most, cuts=(), kind=jnp.bfloat16):
    array = jax.random.normal(own_key, extent, jnp.float32) * width
    if len(cuts) > 0:
        array = levels(own_key, extent, cuts, -0.22, 0.18) * array
    return jnp.clip(array, min=-most, max=most).astype(kind)


def setup_inputs(seed: int = 0) -> dict:
    key_of = jax.random.split(jax.random.key(seed), 7)
    tokens = noise(key_of[0], (TOKENS, D), 1.0, 6.0, ((0, 256),))
    cotangent = noise(key_of[1], (TOKENS, D), 1.0, 6.0, ((0, 256),))
    expert_ids_keys = jax.random.split(jax.random.fold_in(key_of[2], 1), TOKENS // TOK_DEV)
    expert_ids_turns = jax.random.permutation(jax.random.fold_in(key_of[2], 3), TOKENS // TOK_DEV)
    expert_ids = jax.vmap(lambda own, number: shared_out(jax.random.fold_in(key_of[2], 2), own, number, TOK_DEV, EXPERTS, TOP, CAP, 2))(expert_ids_keys, expert_ids_turns).reshape((TOKENS, TOP))
    combine = jnp.clip(jnp.exp(math.log(0.5) - 3.224016 * jax.random.uniform(key_of[3], (TOKENS, TOP), jnp.float32) ** levels(key_of[3], (TOKENS, TOP), ((0, 256),), -0.2, 0.2)), 0.019897461, 0.5).astype(jnp.bfloat16)
    gate_up = noise(key_of[4], (EXPERTS, D, 2 * H), D ** -0.5, 0.125, ((0, 64),))
    down_proj = noise(key_of[5], (EXPERTS, D, H), H ** -0.5, 0.21875, ((0, 64),))
    return dict(tokens=tokens, cotangent=cotangent, expert_ids=expert_ids, combine=combine, gate_up=gate_up, down_proj=down_proj)


def expert_pass(in_rows, cot_rows, weight_rows, w_in, w_out):
    hidden = w_out.shape[1]
    both = jnp.dot(in_rows, w_in, preferred_element_type=jnp.float32)
    gate = both[:, :hidden]
    upper = both[:, hidden:]
    sigma = jax.nn.sigmoid(gate)
    swish = gate * sigma
    activ = (swish * upper).astype(jnp.bfloat16)
    expert_out = lax.dot_general(activ, w_out, (((1,), (1,)), ((), ())), preferred_element_type=jnp.float32).astype(jnp.bfloat16)
    inner = jnp.sum(cot_rows.astype(jnp.float32) * expert_out.astype(jnp.float32), axis=1).astype(jnp.bfloat16)
    grad_rows = (weight_rows[:, None].astype(jnp.float32) * cot_rows.astype(jnp.float32)).astype(jnp.bfloat16)
    grad_act = jnp.dot(grad_rows, w_out, preferred_element_type=jnp.float32)
    grad_gate = grad_act * upper * sigma * (1.0 + gate * (1.0 - sigma))
    grad_upper = grad_act * swish
    grad_both = jnp.concatenate([grad_gate, grad_upper], axis=1).astype(jnp.bfloat16)
    row_grad = lax.dot_general(grad_both, w_in, (((1,), (1,)), ((), ())), preferred_element_type=jnp.float32).astype(jnp.bfloat16)
    grad_in_w = lax.dot_general(in_rows, grad_both, (((0,), (0,)), ((), ())), preferred_element_type=jnp.float32)
    grad_out_w = lax.dot_general(grad_rows, activ, (((0,), (0,)), ((), ())), preferred_element_type=jnp.float32)
    return row_grad, inner, grad_in_w, grad_out_w


def reference(tokens, cotangent, expert_ids, combine, gate_up, down_proj):
    pair_count = TOKENS * TOP
    most_rows = N_EXPERT * N_DP * CAP
    flat_ids = expert_ids.reshape(-1).astype(jnp.int32)
    order = jnp.argsort(flat_ids, stable=True).astype(jnp.int32)
    counts = jnp.bincount(flat_ids, length=EXPERTS).astype(jnp.int32)
    offsets = (jnp.cumsum(counts) - counts).astype(jnp.int32)
    padded = jnp.concatenate([order, jnp.zeros((most_rows,), jnp.int32)])
    flat_comb = combine.reshape(-1)

    def one_expert(carry, inputs):
        grad_acc, inner_acc = carry
        expert, w_in, w_out = inputs
        first_row = offsets[expert]
        picked = lax.dynamic_slice_in_dim(padded, first_row, most_rows)
        valid = jnp.arange(most_rows, dtype=jnp.int32) < counts[expert]
        pair_idx = jnp.where(valid, picked, 0).astype(jnp.int32)
        token_idx = (pair_idx // TOP).astype(jnp.int32)
        in_rows = jnp.where(valid[:, None], tokens[token_idx], jnp.zeros((), jnp.bfloat16))
        cot_rows = jnp.where(valid[:, None], cotangent[token_idx], jnp.zeros((), jnp.bfloat16))
        weight_rows = jnp.where(valid, flat_comb[pair_idx], jnp.zeros((), jnp.bfloat16))
        row_grad, inner, grad_in_w, grad_out_w = expert_pass(in_rows, cot_rows, weight_rows, w_in, w_out)
        grad_acc = grad_acc.at[token_idx].add(jnp.where(valid[:, None], row_grad.astype(jnp.float32), jnp.zeros((), jnp.float32)))
        target = jnp.where(valid, pair_idx, pair_count).astype(jnp.int32)
        inner_acc = inner_acc.at[target].set(inner.astype(jnp.float32))
        return (grad_acc, inner_acc), (grad_in_w.astype(jnp.bfloat16), grad_out_w.astype(jnp.bfloat16))

    start = (jnp.zeros((TOKENS, D), jnp.float32), jnp.zeros((pair_count + 1,), jnp.float32))
    (grad_acc, inner_acc), (grad_gate_up, grad_down) = lax.scan(one_expert, start, (jnp.arange(EXPERTS, dtype=jnp.int32), gate_up, down_proj))
    grad_tokens = grad_acc.astype(jnp.bfloat16)
    grad_combine = inner_acc[:pair_count].reshape(TOKENS, TOP).astype(jnp.bfloat16)
    return (grad_tokens, grad_combine, grad_gate_up, grad_down)
```

```python
import jax
import jax.numpy as jnp
from jax import lax
from jax.sharding import PartitionSpec as P

CAP = 8
NEAR = 8


def shards(tokens, cotangent, expert_ids, combine, gate_up, down_proj):
    tok_rows, width = tokens.shape
    experts = lax.axis_size("expert")
    far = experts // NEAR
    hidden = down_proj.shape[2]
    me = lax.axis_index("expert")
    mine = me // NEAR
    lines = [[z * NEAR + i for z in range(far)] for i in range(NEAR)]
    teams = [[z * NEAR + i for i in range(NEAR)] for z in range(far)]
    w_in = gate_up[0]
    w_out = down_proj[0]
    f32 = jnp.float32
    bf16 = jnp.bfloat16

    hit = expert_ids[:, :, None] == jnp.arange(experts, dtype=jnp.int32)[None, None, :]
    routed = jnp.sum(hit.astype(f32), axis=1)
    lower = jnp.tril(jnp.ones((tok_rows, tok_rows), bf16), -1)
    rank = jnp.dot(lower, routed.astype(bf16), preferred_element_type=f32)
    place = (routed * (rank + 1.0)).astype(bf16)
    weight = jnp.sum(jnp.where(hit, combine[:, :, None].astype(f32), 0.0), axis=1).astype(bf16)
    blank = jnp.zeros((tok_rows, 128 - experts), bf16)
    tok_ext = jnp.concatenate([tokens, place, blank], axis=1)
    cot_ext = jnp.concatenate([cotangent, weight, blank], axis=1)

    all_tok = lax.all_gather(tok_ext, "expert", axis_index_groups=lines)
    all_cot = lax.all_gather(cot_ext, "expert", axis_index_groups=lines)
    places = lax.dynamic_slice_in_dim(all_tok[:, :, width:], mine * NEAR, NEAR, axis=2)
    slot = jnp.arange(1, CAP + 1, dtype=bf16)
    pick = (places[:, :, :, None] == slot).astype(bf16).reshape(far, tok_rows, NEAR * CAP)

    def send(everything):
        rows = jnp.einsum("stj,std->sjd", pick, everything, preferred_element_type=f32).astype(bf16)
        rows = rows.reshape(far, NEAR, CAP, everything.shape[2]).transpose(1, 0, 2, 3)
        return lax.all_to_all(
            rows, "expert", split_axis=0, concat_axis=0, tiled=True, axis_index_groups=teams
        ).reshape(NEAR * far * CAP, everything.shape[2])

    in_rows = send(all_tok[:, :, :width])
    got = send(all_cot)
    both = jnp.dot(in_rows, w_in, preferred_element_type=f32)
    gate = both[:, :hidden]
    upper = both[:, hidden:]
    sigma = jax.nn.sigmoid(gate)
    swish = gate * sigma
    activ = (swish * upper).astype(bf16)
    expert_out = lax.dot_general(
        activ, w_out, (((1,), (1,)), ((), ())), preferred_element_type=f32
    ).astype(bf16)
    cot_rows = got[:, :width]
    own = jnp.arange(128, dtype=jnp.int32)[None, :] == me
    row_weight = jnp.sum(jnp.where(own, got[:, width:].astype(f32), 0.0), axis=1, keepdims=True)
    inner = jnp.sum(cot_rows.astype(f32) * expert_out.astype(f32), axis=1, keepdims=True)
    inner_ext = jnp.where(own, inner, 0.0).astype(bf16)
    grad_rows = (row_weight * cot_rows.astype(f32)).astype(bf16)
    grad_act = jnp.dot(grad_rows, w_out, preferred_element_type=f32)
    grad_gate = grad_act * upper * sigma * (1.0 + gate * (1.0 - sigma))
    grad_upper = grad_act * swish
    grad_both = jnp.concatenate([grad_gate, grad_upper], axis=1).astype(bf16)
    row_grad = lax.dot_general(
        grad_both, w_in, (((1,), (1,)), ((), ())), preferred_element_type=f32
    ).astype(bf16)
    term_in = lax.dot_general(
        in_rows, grad_both, (((0,), (0,)), ((), ())), preferred_element_type=f32
    ).astype(bf16)
    term_out = lax.dot_general(
        grad_rows, activ, (((0,), (0,)), ((), ())), preferred_element_type=f32
    ).astype(bf16)
    grad_gate_up = lax.psum_scatter(term_in, "dp", scatter_dimension=0, tiled=True)[None]
    grad_down = lax.psum_scatter(term_out, "dp", scatter_dimension=0, tiled=True)[None]

    back = jnp.concatenate([row_grad, inner_ext], axis=1)
    back = lax.all_to_all(
        back.reshape(NEAR, far * CAP, width + 128),
        "expert",
        split_axis=0,
        concat_axis=0,
        tiled=True,
        axis_index_groups=teams,
    ).reshape(NEAR, far, CAP, width + 128)
    back = back.transpose(1, 0, 2, 3).reshape(far, NEAR * CAP, width + 128)
    part = jnp.einsum("stj,sjd->std", pick, back, preferred_element_type=f32).astype(bf16)
    part = lax.all_to_all(
        part, "expert", split_axis=0, concat_axis=0, tiled=True, axis_index_groups=lines
    )
    total = jnp.sum(part.astype(f32), axis=0)
    grad_tokens = total[:, :width].astype(bf16)
    inners = total[:, width : width + experts]
    grad_combine = jnp.sum(jnp.where(hit, inners[:, None, :], 0.0), axis=2).astype(bf16)
    return (grad_tokens, grad_combine, grad_gate_up, grad_down)


def solution(mesh):
    in_specs = (
        P(("expert", "dp"), None),
        P(("expert", "dp"), None),
        P(("expert", "dp"), None),
        P(("expert", "dp"), None),
        P("expert", None, None),
        P("expert", None, None),
    )
    out_specs = (
        P(("expert", "dp"), None),
        P(("expert", "dp"), None),
        P("expert", "dp", None),
        P("expert", "dp", None),
    )
    return jax.shard_map(shards, mesh=mesh, in_specs=in_specs, out_specs=out_specs, check_vma=False)
```
